256 devices in a mesh: tile: 64 (over y, z, core), cuts: 4 (over x).
Axes of the slice: x: 4, y: 4, z: 8, core: 2. Of those that a mesh axis runs over, the one named last changes fastest.
Arguments:
- object_slices: float32 [8, 2, 16384, 256], P('cuts', None, 'tile'), may hold values from -1 to 1, as said below
- probe_field: float32 [2, 256, 256], replicated, may hold values from -6 to 6
- row_offsets: int32 [256], P('tile'), may hold values from 0 to 255, as said below
- columns: int32 [256], P('tile'), may hold values from 0 to 0
- counts: int32 [64], P('tile'), may hold values from 1 to 4, 128 in all
- amplitudes: bfloat16 [256, 256, 256], P('tile'), may hold values from 0.25 to 4
Outputs:
- new_object: float32 [8, 2, 16384, 256], P('cuts', None, 'tile')
The draws below stay inside these ranges and needn't reach their ends.
Inputs may be any that keep to these rules, and one draw needn't show every extreme that they name: `row_offsets`: the patch of slot k of block b starts at object row b * 256 + value; in the last block values are at most 0, so every patch lies inside the object and inside its own tile and the next one. `counts`: block b uses its first value slots; the others are padding. The values sum to 128. `object_slices`: every entry has magnitude at most 1.
All inputs are finite; a program needn't handle non-finite values.
Results may differ from the reference program's by a relative error of at most 0.015.
Values may be sent and summed in bfloat16 or wider, within the bound.
No kernel may reach another device: no remote copies, remote signals or barrier semaphores. Data moves between devices by JAX's collectives and lax.ppermute only.
A program may use at most 64 MiB of HBM per device.

```python
import math
import jax
import jax.numpy as jnp
import numpy as np
from jax import lax

PAT = 256
TR = 256
OW = 256
CAP = 4
ITERS = 2
TILES = 64
SLICES = 8


def draw_object_slices(key, part):
    first_key, second_key = jax.random.split(jax.random.fold_in(key, 11))
    shape = (SLICES, TILES * TR, OW)
    magnitude = jax.random.uniform(first_key, shape, jnp.float32, 0.75, 1.0)
    phase = jax.random.uniform(second_key, shape, jnp.float32, -math.pi, math.pi)
    return jnp.stack([magnitude * jnp.cos(phase), magnitude * jnp.sin(phase)], axis=1)


def draw_row_offsets(key, part):
    block = jnp.arange(TILES * CAP, dtype=jnp.int32) // CAP
    upper = jnp.where(block == TILES - 1, TR - PAT + 1, TR).astype(jnp.int32)
    values = jax.random.randint(jax.random.fold_in(key, 23), (TILES * CAP,), 0, upper, dtype=jnp.int32)
    values = values.at[0].set(0)
    return values.at[1].set(TR - 1)


def draw_columns(key, part):
    values = jax.random.randint(jax.random.fold_in(key, 37), (TILES * CAP,), 0, OW - PAT + 1, dtype=jnp.int32)
    values = values.at[0].set(0)
    return values.at[1].set(OW - PAT)


def level_of(own_key, dims, cuts, least, top_value):
    def one(dim, shards_of):
        draws = jax.random.uniform(jax.random.fold_in(jax.random.fold_in(own_key, 6), dim), (shards_of,), jnp.float32, least / len(cuts), top_value / len(cuts))
        return jnp.repeat(jnp.exp(draws), dims[dim] // shards_of).reshape((-1,) + (1,) * (len(dims) - dim - 1))

    level = one(*cuts[0])
    for cut in cuts[1:]:
        level = level * one(*cut)
    return level


def length_profile(count, total, bound, skew):
    weights = [(1 << 20) // math.isqrt(rank ** skew) + 1 for rank in range(2, count + 1)]
    surplus, given = total - bound - (count - 1), [1] * (count - 1)
    while surplus > 0:
        free = [i for i in range(count - 1) if given[i] < bound]
        mass, remaining = sum([weights[i] for i in free]), surplus
        for i in free:
            extra = min(bound - given[i], max(1, remaining * weights[i] // mass), surplus)
            given[i] = given[i] + extra
            surplus = surplus - extra
    return np.array([bound] + given)


def ragged_sizes(rng, number_of, total, limit, lean):
    if number_of == 2:
        one = jax.random.randint(rng, (), max(1, total - limit), min(limit, total - 1) + 1)
        return jnp.stack([one, total - one])
    tallies = jnp.asarray(length_profile(number_of, total, limit, lean), jnp.int32)
    twos = (number_of - 1) // 2
    donor, receiver = tallies[1:1 + 2 * twos:2], tallies[2:2 + 2 * twos:2]
    slack = jnp.minimum(donor - 1, limit - receiver)
    passed = jax.random.randint(jax.random.fold_in(rng, 1), (twos,), 0, 1 << 20) % (slack + 1)
    tallies = tallies.at[1:1 + 2 * twos:2].set(donor - passed).at[2:2 + 2 * twos:2].set(receiver + passed)
    return tallies[jax.random.permutation(jax.random.fold_in(rng, 2), number_of)]


def bell_draw(rng, extent, spread, most, kind=jnp.bfloat16):
    entries = jax.random.normal(rng, extent, jnp.float32) * spread
    return jnp.minimum(jnp.maximum(entries, -most), most).astype(kind)


def setup_inputs(seed: int = 0) -> dict:
    key_of = jax.random.split(jax.random.key(seed), 7)
    object_slices = draw_object_slices(jax.random.fold_in(key_of[6], 71), 0)
    probe_field = bell_draw(key_of[1], (2, PAT, PAT), 1.0, 6.0, jnp.float32)
    row_offsets = draw_row_offsets(jax.random.fold_in(key_of[6], 71), 0)
    columns = draw_columns(jax.random.fold_in(key_of[6], 71), 0)
    counts = ragged_sizes(key_of[4], TILES, TILES * CAP // 2, CAP, 2).astype(jnp.int32)
    amplitudes = jnp.clip(jnp.exp(math.log(4.0) - 2.7725887 * jax.random.uniform(key_of[5], (TILES * CAP, PAT, PAT), jnp.float32) ** level_of(key_of[5], (TILES * CAP, PAT, PAT), ((0, 64),), -0.2, 0.2)), 0.25, 4.0).astype(jnp.bfloat16)
    return {"object_slices": object_slices, "probe_field": probe_field, "row_offsets": row_offsets, "columns": columns, "counts": counts, "amplitudes": amplitudes}


object_rate = 0.25

def tables(size):
    index = jnp.arange(size, dtype=jnp.int32)
    angle = (index[:, None] * index[None, :] % size).astype(jnp.float32) * (2.0 * math.pi / size)
    cosine = jnp.cos(angle)
    sine = jnp.sin(angle)
    signed = jnp.where(index < size // 2, index, index - size)
    phase = (signed * signed % (8 * size)).astype(jnp.float32) * (-math.pi / (4.0 * size))
    filter_re = jnp.cos(phase)
    filter_im = jnp.sin(phase)
    highest = lax.Precision.HIGHEST
    kernel_re = (jnp.dot(filter_re, cosine, precision=highest) - jnp.dot(filter_im, sine, precision=highest)) / size
    kernel_im = (jnp.dot(filter_re, sine, precision=highest) + jnp.dot(filter_im, cosine, precision=highest)) / size
    offset = (index[:, None] - index[None, :]) % size
    norm_factor = 1.0 / math.sqrt(size)
    return ((cosine * norm_factor).astype(jnp.bfloat16), (-sine * norm_factor).astype(jnp.bfloat16), kernel_re[offset].astype(jnp.bfloat16), kernel_im[offset].astype(jnp.bfloat16))

def through(real_table, imag_table, field_re, field_im):
    highest = lax.Precision.HIGHEST
    table_re = real_table.astype(jnp.float32)
    table_im = imag_table.astype(jnp.float32)
    field_re = field_re.astype(jnp.float32)
    field_im = field_im.astype(jnp.float32)
    left = lambda table, field: jnp.einsum('ab,nbc->nac', table, field, precision=highest)
    right = lambda field, table: jnp.einsum('nab,bc->nac', field, table, precision=highest)
    inner_re = left(table_re, field_re) - left(table_im, field_im)
    inner_im = left(table_re, field_im) + left(table_im, field_re)
    inner_re = lax.optimization_barrier(inner_re.astype(jnp.bfloat16)).astype(jnp.float32)
    inner_im = lax.optimization_barrier(inner_im.astype(jnp.bfloat16)).astype(jnp.float32)
    outer_re = right(inner_re, table_re) - right(inner_im, table_im)
    outer_im = right(inner_re, table_im) + right(inner_im, table_re)
    return (outer_re, outer_im)

def propagate(real_table, imag_table, stacked):
    out_re, out_im = through(real_table, imag_table, stacked[:, 0], stacked[:, 1])
    return jnp.stack([out_re, out_im], axis=1).astype(jnp.bfloat16)

def block_pass(current, probe, offsets, cols, count, amps, block, tabs):
    four_re, four_im, kernel_re, kernel_im = tabs
    zero = jnp.zeros((), jnp.int32)
    rows = (block * TR + offsets).astype(jnp.int32)
    windows = jax.vmap(lambda row_start, column: lax.dynamic_slice(current, (zero, zero, row_start.astype(jnp.int32), column.astype(jnp.int32)), (SLICES, 2, PAT, PAT)))(rows, cols)
    mask = (jnp.arange(CAP, dtype=jnp.int32) < count).astype(jnp.float32)
    field = jnp.broadcast_to(probe.astype(jnp.bfloat16)[None], (CAP, 2, PAT, PAT))
    saved = []
    product = field
    for layer_index in range(SLICES):
        saved.append(field)
        window = windows[:, layer_index]
        field32 = field.astype(jnp.float32)
        real = field32[:, 0] * window[:, 0] - field32[:, 1] * window[:, 1]
        imag = field32[:, 0] * window[:, 1] + field32[:, 1] * window[:, 0]
        product = jnp.stack([real, imag], axis=1).astype(jnp.bfloat16)
        if layer_index < SLICES - 1:
            field = propagate(kernel_re, kernel_im, product)
    far_re, far_im = through(four_re, four_im, product[:, 0], product[:, 1])
    modulus = jnp.sqrt(far_re * far_re + far_im * far_im + 1.0)
    factor = mask[:, None, None] * (1.0 - amps.astype(jnp.float32) / modulus)
    chi = jnp.stack([far_re * factor, far_im * factor], axis=1).astype(jnp.bfloat16)
    gradient = propagate(four_re, -four_im, chi)
    terms = [None] * SLICES
    for layer_index in reversed(range(SLICES)):
        field32 = saved[layer_index].astype(jnp.float32)
        grad32 = gradient.astype(jnp.float32)
        window = windows[:, layer_index]
        terms[layer_index] = jnp.stack([field32[:, 0] * grad32[:, 0] + field32[:, 1] * grad32[:, 1], field32[:, 0] * grad32[:, 1] - field32[:, 1] * grad32[:, 0]], axis=1)
        if layer_index > 0:
            adjoint = jnp.stack([window[:, 0] * grad32[:, 0] + window[:, 1] * grad32[:, 1], window[:, 0] * grad32[:, 1] - window[:, 1] * grad32[:, 0]], axis=1)
            gradient = propagate(kernel_re, -kernel_im, adjoint.astype(jnp.bfloat16))
    patch_grads = jnp.stack(terms, axis=1)
    return (patch_grads, rows)

def reference(object_slices, probe_field, row_offsets, columns, counts, amplitudes):
    tabs = tables(PAT)
    offsets = row_offsets.reshape(TILES, CAP).astype(jnp.int32)
    cols = columns.reshape(TILES, CAP).astype(jnp.int32)
    amps = amplitudes.reshape(TILES, CAP, PAT, PAT)
    current = object_slices
    probe = probe_field
    zero = jnp.zeros((), jnp.int32)
    for iteration in range(ITERS):

        def scan_tile(grads, inputs, current=current):
            block, block_offsets, block_cols, count, block_amps = inputs
            patch_grads, rows = block_pass(current, probe, block_offsets, block_cols, count, block_amps, block, tabs)

            def add_patch(slot, grads):
                corner = (zero, zero, rows[slot].astype(jnp.int32), block_cols[slot].astype(jnp.int32))
                region = lax.dynamic_slice(grads, corner, (SLICES, 2, PAT, PAT)) + patch_grads[slot]
                return lax.dynamic_update_slice(grads, region, corner)
            grads = lax.fori_loop(0, CAP, add_patch, grads)
            return (grads, None)
        start = jnp.zeros(current.shape, current.dtype)
        grads, unused = lax.scan(scan_tile, start, (jnp.arange(TILES, dtype=jnp.int32), offsets, cols, counts.astype(jnp.int32), amps))
        current = current - object_rate * grads
    return current
```

```python
from functools import partial
import math

import jax
import jax.numpy as jnp
import numpy as np
from jax import lax
from jax.experimental import pallas as pl
from jax.experimental.pallas import tpu as pltpu
from jax.sharding import PartitionSpec as P

PAT = 256
ITERS = 2
CUTS = 4
LOCAL = 2
TILE = 8
SLICES = CUTS * LOCAL

object_rate = 0.25


f32 = jnp.float32
bf16 = jnp.bfloat16
VMEM = pltpu.MemorySpace.VMEM
SMEM = pltpu.MemorySpace.SMEM


def tables(size):
    index = np.arange(size)
    angle = (index[:, None] * index[None, :] % size) * (2.0 * math.pi / size)
    cosine, sine = np.cos(angle), np.sin(angle)
    signed = np.where(index < size // 2, index, index - size)
    phase = (signed * signed % (8 * size)) * (-math.pi / (4.0 * size))
    filter_re, filter_im = np.cos(phase), np.sin(phase)
    kernel_re = (filter_re @ cosine - filter_im @ sine) / size
    kernel_im = (filter_re @ sine + filter_im @ cosine) / size
    offset = (index[:, None] - index[None, :]) % size
    norm = 1.0 / math.sqrt(size)
    four = np.stack([cosine * norm, -sine * norm])
    kern = np.stack([kernel_re[offset], kernel_im[offset]])
    return np.stack([four, kern]).astype(np.float32).astype(bf16)


def shift(block, axis, distance):
    size = lax.axis_size(axis)
    return lax.ppermute(block, axis, [(i, (i + distance) % size) for i in range(size)])


def step(block, axis, distance):
    devices = range(lax.axis_size(axis))
    route = [(i - distance, i) for i in devices if i - distance in devices]
    return lax.ppermute(block, axis, route)


def split_row(row):
    rest = lax.rem(row, TILE)
    return pl.multiple_of(row - rest, TILE), rest


def cut_windows(extended, offsets_ref, outs):
    for d in range(CUTS):
        base, rest = split_row(offsets_ref[d])
        for i in range(LOCAL):
            for j in range(2):
                rows = extended[i, j, pl.ds(base, PAT + TILE), :]
                rows = pltpu.roll(rows, lax.rem(PAT + TILE - rest, PAT + TILE), 0)
                outs[d][i, j] = rows[:PAT].astype(bf16)


def pack_kernel(offsets_ref, own_ref, margin_ref, *rest):
    outs, extended = rest[:CUTS], rest[CUTS]
    extended[:, :, :PAT, :] = own_ref[...]
    extended[:, :, PAT : 2 * PAT, :] = margin_ref[...].astype(f32)
    cut_windows(extended, offsets_ref, outs)


def update_kernel(
    offsets_ref, own_ref, margin_ref, sum_ref, spill_ref, spill_in_ref, sum_in_ref, *rest
):
    new_ref, outs, extended = rest[0], rest[1 : 1 + CUTS], rest[1 + CUTS]
    fresh = own_ref[...] - object_rate * (sum_ref[...] + spill_in_ref[...].astype(f32))
    new_ref[...] = fresh
    extended[:, :, :PAT, :] = fresh
    extended[:, :, PAT : 2 * PAT, :] = margin_ref[...].astype(f32) - object_rate * (
        sum_in_ref[...].astype(f32) + spill_ref[...].astype(f32)
    )
    cut_windows(extended, offsets_ref, outs)


def sum_kernel(offsets_ref, *rest):
    parts, sum_ref, sum16_ref, spill_ref, total = rest[:CUTS], *rest[CUTS:]
    total[...] = jnp.zeros(total.shape, f32)
    for d in range(CUTS):
        base, rest = split_row(offsets_ref[d])
        for i in range(LOCAL):
            for j in range(2):
                part = jnp.concatenate([parts[d][i, j].astype(f32), jnp.zeros((TILE, PAT), f32)])
                rows = pl.ds(base, PAT + TILE)
                total[i, j, rows, :] = total[i, j, rows, :] + pltpu.roll(part, rest, 0)
    own = total[:, :, :PAT, :]
    sum_ref[...] = own
    sum16_ref[...] = own.astype(bf16)
    spill_ref[...] = total[:, :, PAT : 2 * PAT, :].astype(bf16)


def finish_kernel(own_ref, sum_ref, spill_in_ref, new_ref):
    new_ref[...] = own_ref[...] - object_rate * (sum_ref[...] + spill_in_ref[...].astype(f32))


def transform(left, right, field, inner):
    mid = jnp.dot(left[...], field[...], preferred_element_type=f32)
    inner[:, :PAT] = mid[:PAT].astype(bf16)
    inner[:, PAT:] = mid[PAT:].astype(bf16)
    return jnp.dot(inner[...], right[...], preferred_element_type=f32)


def slot_kernel(scalars_ref, tables_ref, probe_ref, amplitude_ref, *rest):
    sources, results = rest[:CUTS], rest[CUTS : 2 * CUTS]
    window, saved, terms, field, grad, inner, mats, in_sem, out_sem = rest[2 * CUTS :]
    cut = scalars_ref[0]
    live = scalars_ref[1]
    arrivals = []
    for d in range(CUTS):
        copy = pltpu.make_async_copy(
            sources[d], window.at[lax.rem(cut - d + CUTS, CUTS)], in_sem.at[d]
        )
        copy.start()
        arrivals.append(copy)

    @pl.when(live == 0)
    def _():
        terms[...] = jnp.zeros(terms.shape, bf16)

    @pl.when(live != 0)
    def _():
        for t in range(2):
            re, im = tables_ref[t, 0], tables_ref[t, 1]
            for m, sign in ((2 * t, -im), (2 * t + 1, im)):
                mats[m, :PAT, :PAT] = re
                mats[m, :PAT, PAT:] = sign
                mats[m, PAT:, :PAT] = -sign
                mats[m, PAT:, PAT:] = re
        saved[0, :PAT] = probe_ref[0].astype(bf16)
        saved[0, PAT:] = probe_ref[1].astype(bf16)

    for copy in arrivals:
        copy.wait()

    @pl.when(live != 0)
    def _():
        four_left, four_right, kern_left, kern_right = (mats.at[m] for m in range(4))

        def multiply(s):
            re = saved[s, :PAT].astype(f32)
            im = saved[s, PAT:].astype(f32)
            w_re = window[s // LOCAL, s % LOCAL, 0].astype(f32)
            w_im = window[s // LOCAL, s % LOCAL, 1].astype(f32)
            field[:PAT] = (re * w_re - im * w_im).astype(bf16)
            field[PAT:] = (re * w_im + im * w_re).astype(bf16)

        def forward(s, carry):
            multiply(s)
            out = transform(kern_left, kern_right, field, inner)
            saved[s + 1, :PAT] = out[:, :PAT].astype(bf16)
            saved[s + 1, PAT:] = out[:, PAT:].astype(bf16)
            return carry

        lax.fori_loop(0, SLICES - 1, forward, 0)
        multiply(SLICES - 1)
        far = transform(four_left, four_right, field, inner)
        far_re, far_im = far[:, :PAT], far[:, PAT:]
        scale = lax.rsqrt(far_re * far_re + far_im * far_im + 1.0)
        factor = 1.0 - amplitude_ref[0].astype(f32) * scale
        field[:PAT] = (far_re * factor).astype(bf16)
        field[PAT:] = (far_im * factor).astype(bf16)
        out = transform(four_right, four_left, field, inner)
        grad[:PAT] = out[:, :PAT].astype(bf16)
        grad[PAT:] = out[:, PAT:].astype(bf16)

        def term(s):
            g_re = grad[:PAT].astype(f32)
            g_im = grad[PAT:].astype(f32)
            re = saved[s, :PAT].astype(f32)
            im = saved[s, PAT:].astype(f32)
            terms[s // LOCAL, s % LOCAL, 0] = (re * g_re + im * g_im).astype(bf16)
            terms[s // LOCAL, s % LOCAL, 1] = (re * g_im - im * g_re).astype(bf16)
            return g_re, g_im

        def backward(i, carry):
            s = SLICES - 1 - i
            g_re, g_im = term(s)
            w_re = window[s // LOCAL, s % LOCAL, 0].astype(f32)
            w_im = window[s // LOCAL, s % LOCAL, 1].astype(f32)
            field[:PAT] = (w_re * g_re + w_im * g_im).astype(bf16)
            field[PAT:] = (w_re * g_im - w_im * g_re).astype(bf16)
            out = transform(kern_right, kern_left, field, inner)
            grad[:PAT] = out[:, :PAT].astype(bf16)
            grad[PAT:] = out[:, PAT:].astype(bf16)
            return carry

        lax.fori_loop(0, SLICES - 1, backward, 0)
        term(0)

    departures = []
    for d in range(CUTS):
        copy = pltpu.make_async_copy(
            terms.at[lax.rem(cut + d, CUTS)], results[d], out_sem.at[d]
        )
        copy.start()
        departures.append(copy)
    for copy in departures:
        copy.wait()


BLOCK = (LOCAL, 2, PAT, PAT)
LONG = (LOCAL, 2, 2 * PAT, PAT)
block16 = jax.ShapeDtypeStruct(BLOCK, bf16)
block32 = jax.ShapeDtypeStruct(BLOCK, f32)


def vmem(count):
    return [pl.BlockSpec(memory_space=VMEM)] * count


def smem(count=1):
    return [pl.BlockSpec(memory_space=SMEM)] * count


def anywhere(count):
    return [pl.BlockSpec(memory_space=pl.ANY)] * count


def pack(offsets, own, margin):
    return pl.pallas_call(
        pack_kernel,
        out_shape=[block16] * CUTS,
        in_specs=smem() + vmem(2),
        out_specs=vmem(CUTS),
        scratch_shapes=[pltpu.VMEM(LONG, f32)],
    )(offsets, own, margin)


def update(offsets, *arrays):
    return pl.pallas_call(
        update_kernel,
        out_shape=[block32] + [block16] * CUTS,
        in_specs=smem() + vmem(6),
        out_specs=vmem(1 + CUTS),
        scratch_shapes=[pltpu.VMEM(LONG, f32)],
    )(offsets, *arrays)


def add_up(offsets, parts):
    return pl.pallas_call(
        sum_kernel,
        out_shape=[block32, block16, block16],
        in_specs=smem() + vmem(CUTS),
        out_specs=vmem(3),
        scratch_shapes=[pltpu.VMEM(LONG, f32)],
    )(offsets, *parts)


def finish(own, total, spill_in):
    return pl.pallas_call(
        finish_kernel, out_shape=block32, in_specs=vmem(3), out_specs=vmem(1)[0]
    )(own, total, spill_in)


def run_slot(scalars, tabs, probe, amplitudes, windows):
    whole = lambda rank: lambda i, ref: (0,) * rank
    grid_spec = pltpu.PrefetchScalarGridSpec(
        num_scalar_prefetch=1,
        grid=(1,),
        in_specs=[
            pl.BlockSpec((2, 2, PAT, PAT), whole(4)),
            pl.BlockSpec((2, PAT, PAT), whole(3)),
            pl.BlockSpec((1, PAT, PAT), lambda i, ref: (ref[0], 0, 0)),
        ]
        + anywhere(CUTS),
        out_specs=anywhere(CUTS),
        scratch_shapes=[
            pltpu.VMEM((CUTS,) + BLOCK, bf16),
            pltpu.VMEM((SLICES, 2 * PAT, PAT), bf16),
            pltpu.VMEM((CUTS,) + BLOCK, bf16),
            pltpu.VMEM((2 * PAT, PAT), bf16),
            pltpu.VMEM((2 * PAT, PAT), bf16),
            pltpu.VMEM((PAT, 2 * PAT), bf16),
            pltpu.VMEM((4, 2 * PAT, 2 * PAT), bf16),
            pltpu.SemaphoreType.DMA((CUTS,)),
            pltpu.SemaphoreType.DMA((CUTS,)),
        ],
    )
    return pl.pallas_call(slot_kernel, out_shape=[block16] * CUTS, grid_spec=grid_spec)(
        scalars, tabs, probe, amplitudes, *windows
    )


def exchange(blocks):
    return [blocks[0]] + [shift(blocks[d], "cuts", d) for d in range(1, CUTS)]


def local(object_slices, probe_field, row_offsets, columns, counts, amplitudes):
    tabs = jnp.asarray(tables(PAT))
    cut = lax.axis_index("cuts").astype(jnp.int32)
    turn = jnp.arange(CUTS, dtype=jnp.int32)
    ahead = row_offsets[(cut + turn) % CUTS]
    behind = row_offsets[(cut - turn + CUTS) % CUTS]
    live = (cut < counts[0]).astype(jnp.int32)
    scalars = jnp.stack([cut, live])
    own = object_slices
    margin = step(own.astype(bf16), "tile", -1)
    windows = pack(ahead, own, margin)
    for iteration in range(ITERS):
        arrived = exchange(windows)
        terms = run_slot(scalars, tabs, probe_field, amplitudes, arrived)
        parts = exchange(terms)
        total, total16, spill = add_up(behind, parts)
        spill_in = step(spill, "tile", 1)
        if iteration + 1 < ITERS:
            total_in = step(total16, "tile", -1)
            own, *windows = update(ahead, own, margin, total, spill, spill_in, total_in)
        else:
            own = finish(own, total, spill_in)
    return own


def solution(mesh):
    in_specs = (
        P("cuts", None, "tile", None),
        P(),
        P("tile"),
        P("tile"),
        P("tile"),
        P("tile", None, None),
    )
    out_specs = P("cuts", None, "tile", None)
    return jax.shard_map(local, mesh=mesh, in_specs=in_specs, out_specs=out_specs, check_vma=False)
```

```python
from functools import partial
import math

import jax
import jax.numpy as jnp
import numpy as np
from jax import lax
from jax.experimental import pallas as pl
from jax.experimental.pallas import tpu as pltpu
from jax.sharding import PartitionSpec as P


PAT = 256
ITERS = 2
CUTS = 4
LOCAL = 2
SMALL = 4
LARGE = 12
SLICES = CUTS * LOCAL

object_rate = 0.25


f32 = jnp.float32
bf16 = jnp.bfloat16
VMEM = pltpu.MemorySpace.VMEM
SMEM = pltpu.MemorySpace.SMEM


def tables(size):
    index = np.arange(size)
    angle = (index[:, None] * index[None, :] % size) * (2.0 * math.pi / size)
    cosine, sine = np.cos(angle), np.sin(angle)
    signed = np.where(index < size // 2, index, index - size)
    phase = (signed * signed % (8 * size)) * (-math.pi / (4.0 * size))
    filter_re, filter_im = np.cos(phase), np.sin(phase)
    kernel_re = (filter_re @ cosine - filter_im @ sine) / size
    kernel_im = (filter_re @ sine + filter_im @ cosine) / size
    offset = (index[:, None] - index[None, :]) % size
    norm = 1.0 / math.sqrt(size)
    four = np.stack([cosine * norm, -sine * norm])
    kern = np.stack([kernel_re[offset], kernel_im[offset]])
    return np.stack([four, kern]).astype(np.float32).astype(bf16)


def shift(block, axis, distance):
    size = lax.axis_size(axis)
    return lax.ppermute(block, axis, [(i, (i + distance) % size) for i in range(size)])


def step(block, axis, distance):
    devices = range(lax.axis_size(axis))
    route = [(i - distance, i) for i in devices if i - distance in devices]
    return lax.ppermute(block, axis, route)


def chunks(size):
    for m in range(0, PAT, size):
        yield pl.ds(m, size), m + lax.broadcasted_iota(jnp.int32, (size, PAT), 0)


def cut_windows(own, margin, rows, place, offsets_ref, outs, j):
    for d in range(CUTS):
        outs[d][j, place] = jnp.where(rows >= offsets_ref[d], own, margin).astype(bf16)


def pack_kernel(i, offsets_ref, own_ref, margin_ref, *outs):
    for j in range(2):
        for place, rows in chunks(32):
            own = own_ref[i, j, place]
            cut_windows(own, margin_ref[j, place].astype(f32), rows, place, offsets_ref, outs, j)


def update_part(i, offsets_ref, own_ref, margin_ref, sum_ref, spill_ref, spill_in_ref, sum_in_ref,
                new_ref, *outs):
    for j in range(2):
        for place, rows in chunks(32):
            arrived = sum_ref[j, place] + spill_in_ref[j, place].astype(f32)
            own = own_ref[i, j, place] - object_rate * arrived
            new_ref[j, place] = own
            beyond = sum_in_ref[j, place].astype(f32) + spill_ref[j, place].astype(f32)
            margin = margin_ref[j, place].astype(f32) - object_rate * beyond
            cut_windows(own, margin, rows, place, offsets_ref, outs, j)


def sum_part(offsets_ref, *rest):
    parts, sum_ref, sum16_ref, spill_ref = rest[:CUTS], *rest[CUTS:]
    for j in range(2):
        for place, rows in chunks(32):
            own, spill = 0.0, 0.0
            for d in range(CUTS):
                part = parts[d][j, place].astype(f32)
                here = rows >= offsets_ref[d]
                own = own + jnp.where(here, part, 0.0)
                spill = spill + jnp.where(here, 0.0, part)
            sum_ref[j, place] = own
            sum16_ref[j, place] = own.astype(bf16)
            spill_ref[j, place] = spill.astype(bf16)


def middle_kernel(ahead_ref, behind_ref, *rest):
    ins, outs = rest[: 6 + CUTS], rest[6 + CUTS :]
    update_part(0, ahead_ref, *ins[:6], *outs[: 1 + CUTS])
    sum_part(behind_ref, *ins[6:], *outs[1 + CUTS :])


def finish_kernel(*rest):
    new_ref = rest[-1]
    for i in range(LOCAL):
        own_ref, sum_ref, spill_in_ref = rest[3 * i : 3 * i + 3]
        arrived = sum_ref[...] + spill_in_ref[...].astype(f32)
        new_ref[i] = own_ref[...] - object_rate * arrived


def prepare_kernel(scalars_ref, tables_ref, probe_ref, mats_ref, start_ref):
    turn = scalars_ref[2]

    def put(m, re, im):
        mats_ref[m, :PAT, :PAT] = re
        mats_ref[m, :PAT, PAT:] = -im
        mats_ref[m, PAT:, :PAT] = im
        mats_ref[m, PAT:, PAT:] = re

    four_re, four_im = tables_ref[0, 0], tables_ref[0, 1]
    wide_re, wide_im = four_re.astype(f32), four_im.astype(f32)
    put(0, pltpu.roll(wide_re, turn, 1).astype(bf16), pltpu.roll(wide_im, turn, 1).astype(bf16))
    put(1, four_re, -four_im)
    put(2, pltpu.roll(wide_re, turn, 0).astype(bf16), -pltpu.roll(wide_im, turn, 0).astype(bf16))
    put(3, four_re, four_im)
    put(4, tables_ref[1, 0], tables_ref[1, 1])
    put(5, tables_ref[1, 0], -tables_ref[1, 1])
    for j in range(2):
        start_ref[j * PAT : (j + 1) * PAT] = pltpu.roll(probe_ref[j], turn, 0).astype(bf16)


CHUNK = 32


def transform(left, right, field, inner):
    for half in (slice(0, PAT), slice(PAT, 2 * PAT)):
        mid = jnp.dot(left[half], field[...], preferred_element_type=f32)
        inner[:, half] = mid.astype(bf16)
    return [
        jnp.dot(inner[...], right[:, half], preferred_element_type=f32)
        for half in (slice(0, PAT), slice(PAT, 2 * PAT))
    ]


def slot_kernel(scalars_ref, mats, start_ref, amplitudes_ref, *rest):
    count = CUTS * LOCAL
    sources, results = rest[:count], rest[count : 2 * count]
    window, saved, terms, field, inner, amplitude, in_sem, out_sem, side_sem = rest[2 * count :]
    cut = scalars_ref[0]
    live = scalars_ref[1]

    @pl.when(live == 0)
    def _():
        terms[0, 0] = jnp.zeros(PLANE, bf16)
        copies = [
            pltpu.make_async_copy(terms.at[0, 0], results[n], out_sem.at[n]) for n in range(count)
        ]
        for copy in copies:
            copy.start()
        for copy in copies:
            copy.wait()

    @pl.when(live != 0)
    def _():
        side = pltpu.make_async_copy(amplitudes_ref.at[cut], amplitude, side_sem)
        for n in range(count):
            i, d = n // CUTS, n % CUTS
            owner = lax.rem(cut - d + CUTS, CUTS)
            pltpu.make_async_copy(
                sources[n], window.at[owner, i], in_sem.at[owner * LOCAL + i]
            ).start()
        side.start()
        four_in, four_in_right, four_out, four_out_right, kern, kern_conj = (
            mats.at[m] for m in range(6)
        )

        def arrive(s):
            pltpu.make_async_copy(sources[0], window.at[s // LOCAL, s % LOCAL], in_sem.at[s]).wait()

        def leave(s):
            turn = lax.rem(s // LOCAL - cut + CUTS, CUTS)
            for n in range(count):
                i, d = n // CUTS, n % CUTS

                @pl.when((turn == d) & (s % LOCAL == i))
                def _():
                    pltpu.make_async_copy(
                        terms.at[s // LOCAL, s % LOCAL], results[n], out_sem.at[n]
                    ).start()

        def piece(s, m):
            rows = pl.ds(m, CHUNK)
            place = (s // LOCAL, s % LOCAL)
            return window[place + (0, rows)].astype(f32), window[place + (1, rows)].astype(f32)

        def put(m, re, im):
            field[m : m + CHUNK] = re.astype(bf16)
            field[PAT + m : PAT + m + CHUNK] = im.astype(bf16)

        def multiply(s, m, re, im):
            w_re, w_im = piece(s, m)
            put(m, re * w_re - im * w_im, re * w_im + im * w_re)

        def parts(out):
            for m in range(0, PAT, CHUNK):
                yield m, out[0][m : m + CHUNK], out[1][m : m + CHUNK]

        def gather(s, out):
            for m, g_re, g_im in parts(out):
                re = saved[s, m : m + CHUNK].astype(f32)
                im = saved[s, PAT + m : PAT + m + CHUNK].astype(f32)
                place = (s // LOCAL, s % LOCAL)
                rows = pl.ds(m, CHUNK)
                terms[place + (0, rows)] = (re * g_re + im * g_im).astype(bf16)
                terms[place + (1, rows)] = (re * g_im - im * g_re).astype(bf16)
                w_re, w_im = piece(s, m)
                put(m, w_re * g_re + w_im * g_im, w_re * g_im - w_im * g_re)

        saved[0] = start_ref[...]
        arrive(0)
        for m in range(0, PAT, CHUNK):
            re = start_ref[m : m + CHUNK].astype(f32)
            im = start_ref[PAT + m : PAT + m + CHUNK].astype(f32)
            multiply(0, m, re, im)

        def forward(s, carry):
            arrive(s)
            out = transform(kern, kern_conj, field, inner)
            for m, re, im in parts(out):
                saved[s, m : m + CHUNK] = re.astype(bf16)
                saved[s, PAT + m : PAT + m + CHUNK] = im.astype(bf16)
                multiply(s, m, re, im)
            return carry

        lax.fori_loop(1, SLICES, forward, 0)
        side.wait()
        far = transform(four_in, four_in_right, field, inner)
        for m, re, im in parts(far):
            scale = lax.rsqrt(re * re + im * im + 1.0)
            factor = 1.0 - amplitude[m : m + CHUNK].astype(f32) * scale
            put(m, re * factor, im * factor)
        gather(SLICES - 1, transform(four_out, four_out_right, field, inner))
        leave(SLICES - 1)

        def backward(i, carry):
            gather(SLICES - 1 - i, transform(kern_conj, kern, field, inner))
            leave(SLICES - 1 - i)
            return carry

        lax.fori_loop(1, SLICES, backward, 0)
        for n in range(count):
            pltpu.make_async_copy(terms.at[0, 0], results[n], out_sem.at[n]).wait()


PLANE = (2, PAT, PAT)
BLOCK = (LOCAL,) + PLANE
plane16 = jax.ShapeDtypeStruct(PLANE, bf16)
plane32 = jax.ShapeDtypeStruct(PLANE, f32)
block32 = jax.ShapeDtypeStruct(BLOCK, f32)


def limit(mib):
    return pltpu.CompilerParams(vmem_limit_bytes=mib * 1024 * 1024)


def vmem(count):
    return [pl.BlockSpec(memory_space=VMEM)] * count


def smem(count=1):
    return [pl.BlockSpec(memory_space=SMEM)] * count


def anywhere(count):
    return [pl.BlockSpec(memory_space=pl.ANY)] * count


def in_hbm(array):
    return pltpu.with_memory_space_constraint(array, pltpu.MemorySpace.HBM)


def pack(i, offsets, own, margin):
    return pl.pallas_call(
        partial(pack_kernel, i),
        compiler_params=limit(SMALL),
        out_shape=[plane16] * CUTS,
        in_specs=smem() + vmem(2),
        out_specs=vmem(CUTS),
    )(offsets, own, margin)


def update(i, offsets, *arrays):
    return pl.pallas_call(
        partial(update_part, i),
        compiler_params=limit(SMALL),
        out_shape=[plane32] + [plane16] * CUTS,
        in_specs=smem() + vmem(6),
        out_specs=vmem(1 + CUTS),
    )(offsets, *arrays)


def add_up(offsets, parts):
    return pl.pallas_call(
        sum_part,
        compiler_params=limit(SMALL),
        out_shape=[plane32, plane16, plane16],
        in_specs=smem() + vmem(CUTS),
        out_specs=vmem(3),
    )(offsets, *parts)


def middle(ahead, behind, *arrays):
    return pl.pallas_call(
        middle_kernel,
        compiler_params=limit(SMALL),
        out_shape=[plane32] + [plane16] * CUTS + [plane32, plane16, plane16],
        in_specs=smem(2) + vmem(6 + CUTS),
        out_specs=vmem(4 + CUTS),
    )(ahead, behind, *arrays)


def finish(*arrays):
    return pl.pallas_call(
        finish_kernel, compiler_params=limit(SMALL), out_shape=block32, in_specs=vmem(3 * LOCAL), out_specs=vmem(1)[0]
    )(*arrays)


def prepare(scalars, tabs, probe):
    return pl.pallas_call(
        prepare_kernel,
        compiler_params=limit(SMALL),
        out_shape=[
            jax.ShapeDtypeStruct((6, 2 * PAT, 2 * PAT), bf16),
            jax.ShapeDtypeStruct((2 * PAT, PAT), bf16),
        ],
        in_specs=smem() + vmem(2),
        out_specs=vmem(2),
    )(scalars, tabs, probe)


def run_slot(scalars, mats, start, amplitudes, windows):
    count = CUTS * LOCAL
    return pl.pallas_call(
        slot_kernel,
        compiler_params=limit(LARGE),
        out_shape=[plane16] * count,
        in_specs=smem()
        + vmem(2)
        + anywhere(1 + count),
        out_specs=anywhere(count),
        scratch_shapes=[
            pltpu.VMEM((CUTS,) + BLOCK, bf16),
            pltpu.VMEM((SLICES, 2 * PAT, PAT), bf16),
            pltpu.VMEM((CUTS,) + BLOCK, bf16),
            pltpu.VMEM((2 * PAT, PAT), bf16),
            pltpu.VMEM((PAT, 2 * PAT), bf16),
            pltpu.VMEM((PAT, PAT), bf16),
            pltpu.SemaphoreType.DMA((count,)),
            pltpu.SemaphoreType.DMA((count,)),
            pltpu.SemaphoreType.DMA,
        ],
    )(scalars, mats, start, in_hbm(amplitudes), *windows)


def exchange(blocks):
    arrived = [blocks[0]]
    for d in range(1, CUTS):
        arrived.append(shift(blocks[d], "cuts", d))
    return arrived


def run(object_slices, probe_field, row_offsets, columns, counts, amplitudes):
    tabs = jnp.asarray(tables(PAT))
    cut = lax.axis_index("cuts").astype(jnp.int32)
    turn = jnp.arange(CUTS, dtype=jnp.int32)
    ahead = row_offsets[(cut + turn) % CUTS]
    behind = row_offsets[(cut - turn + CUTS) % CUTS]
    live = (cut < counts[0]).astype(jnp.int32)
    scalars = jnp.stack([cut, live, ahead[0]])
    constants = prepare(scalars, tabs, probe_field)
    each = range(LOCAL)
    margins = [step(object_slices[i].astype(bf16), "tile", -1) for i in each]
    windows = []
    for i in each:
        windows += exchange(pack(i, ahead, object_slices, margins[i]))
    for iteration in range(ITERS):
        terms = run_slot(scalars, *constants, amplitudes, windows)
        first, second = (exchange(terms[CUTS * i : CUTS * (i + 1)]) for i in each)
        total_a, total16_a, spill_a = add_up(behind, first)
        spill_in_a = step(spill_a, "tile", 1)
        if iteration + 1 < ITERS:
            total_in_a = step(total16_a, "tile", -1)
            out = middle(
                ahead, behind, object_slices, margins[0], total_a, spill_a, spill_in_a,
                total_in_a, *second
            )
            own_a, cut_a, (total_b, total16_b, spill_b) = out[0], out[1 : 1 + CUTS], out[1 + CUTS :]
            spill_in_b = step(spill_b, "tile", 1)
            total_in_b = step(total16_b, "tile", -1)
            windows = exchange(cut_a)
            own_b, *cut_b = update(
                1, ahead, object_slices, margins[1], total_b, spill_b, spill_in_b, total_in_b
            )
            windows += exchange(cut_b)
            again, own_a = lax.optimization_barrier((scalars, own_a))
            constants = prepare(again, tabs, probe_field)
    total_b, _, spill_b = add_up(behind, second)
    spill_in_b = step(spill_b, "tile", 1)
    return finish(own_a, total_a, spill_in_a, own_b, total_b, spill_in_b)


def solution(mesh):
    in_specs = (
        P("cuts", None, "tile", None),
        P(),
        P("tile"),
        P("tile"),
        P("tile"),
        P("tile", None, None),
    )
    out_specs = P("cuts", None, "tile", None)
    return jax.shard_map(run, mesh=mesh, in_specs=in_specs, out_specs=out_specs, check_vma=False)
```

```python
from functools import partial
import math

import jax
import jax.numpy as jnp
import numpy as np
from jax import lax
from jax.experimental import pallas as pl
from jax.experimental.pallas import tpu as pltpu
from jax.sharding import PartitionSpec as P


PAT = 256
ITERS = 2
CUTS = 4
LOCAL = 2
SMALL = 4
LARGE = 12
SLICES = CUTS * LOCAL

object_rate = 0.25


f32 = jnp.float32
bf16 = jnp.bfloat16
VMEM = pltpu.MemorySpace.VMEM
SMEM = pltpu.MemorySpace.SMEM


def tables(size):
    index = np.arange(size)
    angle = (index[:, None] * index[None, :] % size) * (2.0 * math.pi / size)
    cosine, sine = np.cos(angle), np.sin(angle)
    signed = np.where(index < size // 2, index, index - size)
    phase = (signed * signed % (8 * size)) * (-math.pi / (4.0 * size))
    filter_re, filter_im = np.cos(phase), np.sin(phase)
    kernel_re = (filter_re @ cosine - filter_im @ sine) / size
    kernel_im = (filter_re @ sine + filter_im @ cosine) / size
    offset = (index[:, None] - index[None, :]) % size
    norm = 1.0 / math.sqrt(size)
    four = np.stack([cosine * norm, -sine * norm])
    kern = np.stack([kernel_re[offset], kernel_im[offset]])
    return np.stack([four, kern]).astype(np.float32).astype(bf16)


def shift(block, axis, distance):
    size = lax.axis_size(axis)
    return lax.ppermute(block, axis, [(i, (i + distance) % size) for i in range(size)])


def step(block, axis, distance):
    devices = range(lax.axis_size(axis))
    route = [(i - distance, i) for i in devices if i - distance in devices]
    return lax.ppermute(block, axis, route)


def offset_at(offsets_ref, distance):
    cut = lax.axis_index("cuts").astype(jnp.int32)
    return offsets_ref[lax.rem(cut + distance + CUTS, CUTS)]


def chunks(size):
    for m in range(0, PAT, size):
        yield pl.ds(m, size), m + lax.broadcasted_iota(jnp.int32, (size, PAT), 0)


def cut_windows(own, margin, rows, place, offsets_ref, outs, j):
    for d in range(CUTS):
        outs[d][j, place] = jnp.where(rows >= offset_at(offsets_ref, d), own, margin).astype(bf16)


def cast_kernel(own_ref, *outs):
    for i in range(LOCAL):
        outs[i][...] = own_ref[i].astype(bf16)


def pack_kernel(i, offsets_ref, own_ref, margin_ref, *outs):
    for j in range(2):
        for place, rows in chunks(32):
            own = own_ref[i, j, place]
            cut_windows(own, margin_ref[j, place].astype(f32), rows, place, offsets_ref, outs, j)


def update_part(i, offsets_ref, own_ref, margin_ref, sum_ref, spill_ref, spill_in_ref, sum_in_ref,
                new_ref, *outs):
    for j in range(2):
        for place, rows in chunks(32):
            arrived = sum_ref[j, place] + spill_in_ref[j, place].astype(f32)
            own = own_ref[i, j, place] - object_rate * arrived
            new_ref[j, place] = own
            beyond = sum_in_ref[j, place].astype(f32) + spill_ref[j, place].astype(f32)
            margin = margin_ref[j, place].astype(f32) - object_rate * beyond
            cut_windows(own, margin, rows, place, offsets_ref, outs, j)


def sum_part(offsets_ref, *rest):
    parts, sum_ref, sum16_ref, spill_ref = rest[:CUTS], *rest[CUTS:]
    for j in range(2):
        for place, rows in chunks(32):
            own, spill = 0.0, 0.0
            for d in range(CUTS):
                part = parts[d][j, place].astype(f32)
                here = rows >= offset_at(offsets_ref, -d)
                own = own + jnp.where(here, part, 0.0)
                spill = spill + jnp.where(here, 0.0, part)
            sum_ref[j, place] = own
            sum16_ref[j, place] = own.astype(bf16)
            spill_ref[j, place] = spill.astype(bf16)


def middle_kernel(offsets_ref, *rest):
    ins, outs = rest[: 6 + CUTS], rest[6 + CUTS :]
    update_part(0, offsets_ref, *ins[:6], *outs[: 1 + CUTS])
    sum_part(offsets_ref, *ins[6:], *outs[1 + CUTS :])


def finish_kernel(*rest):
    new_ref = rest[-1]
    for i in range(LOCAL):
        own_ref, sum_ref, spill_in_ref = rest[3 * i : 3 * i + 3]
        arrived = sum_ref[...] + spill_in_ref[...].astype(f32)
        new_ref[i] = own_ref[...] - object_rate * arrived


def prepare_kernel(offsets_ref, tables_ref, probe_ref, mats_ref, start_ref):
    turn = offset_at(offsets_ref, 0)

    def put(m, re, im):
        mats_ref[m, :PAT, :PAT] = re
        mats_ref[m, :PAT, PAT:] = -im
        mats_ref[m, PAT:, :PAT] = im
        mats_ref[m, PAT:, PAT:] = re

    four_re, four_im = tables_ref[0, 0], tables_ref[0, 1]
    wide_re, wide_im = four_re.astype(f32), four_im.astype(f32)
    put(0, pltpu.roll(wide_re, turn, 1).astype(bf16), pltpu.roll(wide_im, turn, 1).astype(bf16))
    put(1, four_re, -four_im)
    put(2, pltpu.roll(wide_re, turn, 0).astype(bf16), -pltpu.roll(wide_im, turn, 0).astype(bf16))
    put(3, four_re, four_im)
    put(4, tables_ref[1, 0], tables_ref[1, 1])
    put(5, tables_ref[1, 0], -tables_ref[1, 1])
    for j in range(2):
        start_ref[j * PAT : (j + 1) * PAT] = pltpu.roll(probe_ref[j], turn, 0).astype(bf16)


CHUNK = 32


def transform(left, right, field, inner):
    for half in (slice(0, PAT), slice(PAT, 2 * PAT)):
        mid = jnp.dot(left[half], field[...], preferred_element_type=f32)
        inner[:, half] = mid.astype(bf16)
    return [
        jnp.dot(inner[...], right[:, half], preferred_element_type=f32)
        for half in (slice(0, PAT), slice(PAT, 2 * PAT))
    ]


def slot_kernel(counts_ref, mats, start_ref, amplitudes_ref, *rest):
    count = CUTS * LOCAL
    sources, results = rest[:count], rest[count : 2 * count]
    window, saved, terms, field, inner, amplitude, in_sem, out_sem, side_sem = rest[2 * count :]
    cut = lax.axis_index("cuts").astype(jnp.int32)
    live = (cut < counts_ref[0]).astype(jnp.int32)

    @pl.when(live == 0)
    def _():
        terms[0, 0] = jnp.zeros(PLANE, bf16)
        copies = [
            pltpu.make_async_copy(terms.at[0, 0], results[n], out_sem.at[n]) for n in range(count)
        ]
        for copy in copies:
            copy.start()
        for copy in copies:
            copy.wait()

    @pl.when(live != 0)
    def _():
        side = pltpu.make_async_copy(amplitudes_ref.at[cut], amplitude, side_sem)
        for n in range(count):
            i, d = n // CUTS, n % CUTS
            owner = lax.rem(cut - d + CUTS, CUTS)
            pltpu.make_async_copy(
                sources[n], window.at[owner, i], in_sem.at[owner * LOCAL + i]
            ).start()
        side.start()
        four_in, four_in_right, four_out, four_out_right, kern, kern_conj = (
            mats.at[m] for m in range(6)
        )

        def arrive(s):
            pltpu.make_async_copy(sources[0], window.at[s // LOCAL, s % LOCAL], in_sem.at[s]).wait()

        def leave(s):
            turn = lax.rem(s // LOCAL - cut + CUTS, CUTS)
            for n in range(count):
                i, d = n // CUTS, n % CUTS

                @pl.when((turn == d) & (s % LOCAL == i))
                def _():
                    pltpu.make_async_copy(
                        terms.at[s // LOCAL, s % LOCAL], results[n], out_sem.at[n]
                    ).start()

        def piece(s, m):
            rows = pl.ds(m, CHUNK)
            place = (s // LOCAL, s % LOCAL)
            return window[place + (0, rows)].astype(f32), window[place + (1, rows)].astype(f32)

        def put(m, re, im):
            field[m : m + CHUNK] = re.astype(bf16)
            field[PAT + m : PAT + m + CHUNK] = im.astype(bf16)

        def multiply(s, m, re, im):
            w_re, w_im = piece(s, m)
            put(m, re * w_re - im * w_im, re * w_im + im * w_re)

        def parts(out):
            for m in range(0, PAT, CHUNK):
                yield m, out[0][m : m + CHUNK], out[1][m : m + CHUNK]

        def gather(s, out):
            for m, g_re, g_im in parts(out):
                re = saved[s, m : m + CHUNK].astype(f32)
                im = saved[s, PAT + m : PAT + m + CHUNK].astype(f32)
                place = (s // LOCAL, s % LOCAL)
                rows = pl.ds(m, CHUNK)
                terms[place + (0, rows)] = (re * g_re + im * g_im).astype(bf16)
                terms[place + (1, rows)] = (re * g_im - im * g_re).astype(bf16)
                w_re, w_im = piece(s, m)
                put(m, w_re * g_re + w_im * g_im, w_re * g_im - w_im * g_re)

        saved[0] = start_ref[...]
        arrive(0)
        for m in range(0, PAT, CHUNK):
            re = start_ref[m : m + CHUNK].astype(f32)
            im = start_ref[PAT + m : PAT + m + CHUNK].astype(f32)
            multiply(0, m, re, im)

        def forward(s, carry):
            arrive(s)
            out = transform(kern, kern_conj, field, inner)
            for m, re, im in parts(out):
                saved[s, m : m + CHUNK] = re.astype(bf16)
                saved[s, PAT + m : PAT + m + CHUNK] = im.astype(bf16)
                multiply(s, m, re, im)
            return carry

        lax.fori_loop(1, SLICES, forward, 0)
        side.wait()
        far = transform(four_in, four_in_right, field, inner)
        for m, re, im in parts(far):
            scale = lax.rsqrt(re * re + im * im + 1.0)
            factor = 1.0 - amplitude[m : m + CHUNK].astype(f32) * scale
            put(m, re * factor, im * factor)
        gather(SLICES - 1, transform(four_out, four_out_right, field, inner))
        leave(SLICES - 1)

        def backward(i, carry):
            gather(SLICES - 1 - i, transform(kern_conj, kern, field, inner))
            leave(SLICES - 1 - i)
            return carry

        lax.fori_loop(1, SLICES, backward, 0)
        for n in range(count):
            pltpu.make_async_copy(terms.at[0, 0], results[n], out_sem.at[n]).wait()


PLANE = (2, PAT, PAT)
BLOCK = (LOCAL,) + PLANE
plane16 = jax.ShapeDtypeStruct(PLANE, bf16)
plane32 = jax.ShapeDtypeStruct(PLANE, f32)
block32 = jax.ShapeDtypeStruct(BLOCK, f32)


def limit(mib):
    return pltpu.CompilerParams(vmem_limit_bytes=mib * 1024 * 1024)


def vmem(count):
    return [pl.BlockSpec(memory_space=VMEM)] * count


def smem(count=1):
    return [pl.BlockSpec(memory_space=SMEM)] * count


def anywhere(count):
    return [pl.BlockSpec(memory_space=pl.ANY)] * count


def in_hbm(array):
    return pltpu.with_memory_space_constraint(array, pltpu.MemorySpace.HBM)


def cast(own):
    return pl.pallas_call(
        cast_kernel,
        compiler_params=limit(SMALL),
        out_shape=[plane16] * LOCAL,
        in_specs=vmem(1),
        out_specs=vmem(LOCAL),
    )(own)


def pack(i, offsets, own, margin):
    return pl.pallas_call(
        partial(pack_kernel, i),
        compiler_params=limit(SMALL),
        out_shape=[plane16] * CUTS,
        in_specs=smem() + vmem(2),
        out_specs=vmem(CUTS),
    )(offsets, own, margin)


def update(i, offsets, *arrays):
    return pl.pallas_call(
        partial(update_part, i),
        compiler_params=limit(SMALL),
        out_shape=[plane32] + [plane16] * CUTS,
        in_specs=smem() + vmem(6),
        out_specs=vmem(1 + CUTS),
    )(offsets, *arrays)


def add_up(offsets, parts):
    return pl.pallas_call(
        sum_part,
        compiler_params=limit(SMALL),
        out_shape=[plane32, plane16, plane16],
        in_specs=smem() + vmem(CUTS),
        out_specs=vmem(3),
    )(offsets, *parts)


def middle(offsets, *arrays):
    return pl.pallas_call(
        middle_kernel,
        compiler_params=limit(SMALL),
        out_shape=[plane32] + [plane16] * CUTS + [plane32, plane16, plane16],
        in_specs=smem() + vmem(6 + CUTS),
        out_specs=vmem(4 + CUTS),
    )(offsets, *arrays)


def finish(*arrays):
    return pl.pallas_call(
        finish_kernel, compiler_params=limit(SMALL), out_shape=block32, in_specs=vmem(3 * LOCAL), out_specs=vmem(1)[0]
    )(*arrays)


def prepare(offsets, tabs, probe):
    return pl.pallas_call(
        prepare_kernel,
        compiler_params=limit(SMALL),
        out_shape=[
            jax.ShapeDtypeStruct((6, 2 * PAT, 2 * PAT), bf16),
            jax.ShapeDtypeStruct((2 * PAT, PAT), bf16),
        ],
        in_specs=smem() + vmem(2),
        out_specs=vmem(2),
    )(offsets, tabs, probe)


def run_slot(counts, mats, start, amplitudes, windows):
    count = CUTS * LOCAL
    return pl.pallas_call(
        slot_kernel,
        compiler_params=limit(LARGE),
        out_shape=[plane16] * count,
        in_specs=smem()
        + vmem(2)
        + anywhere(1 + count),
        out_specs=anywhere(count),
        scratch_shapes=[
            pltpu.VMEM((CUTS,) + BLOCK, bf16),
            pltpu.VMEM((SLICES, 2 * PAT, PAT), bf16),
            pltpu.VMEM((CUTS,) + BLOCK, bf16),
            pltpu.VMEM((2 * PAT, PAT), bf16),
            pltpu.VMEM((PAT, 2 * PAT), bf16),
            pltpu.VMEM((PAT, PAT), bf16),
            pltpu.SemaphoreType.DMA((count,)),
            pltpu.SemaphoreType.DMA((count,)),
            pltpu.SemaphoreType.DMA,
        ],
    )(counts, mats, start, in_hbm(amplitudes), *windows)


def exchange(blocks):
    arrived = [blocks[0]]
    for d in range(1, CUTS):
        arrived.append(shift(blocks[d], "cuts", d))
    return arrived


def run(object_slices, probe_field, row_offsets, columns, counts, amplitudes):
    tabs = jnp.asarray(tables(PAT))
    constants = prepare(row_offsets, tabs, probe_field)
    each = range(LOCAL)
    margins = [step(rows, "tile", -1) for rows in cast(object_slices)]
    windows = []
    for i in each:
        windows += exchange(pack(i, row_offsets, object_slices, margins[i]))
    for iteration in range(ITERS):
        terms = run_slot(counts, *constants, amplitudes, windows)
        first, second = (exchange(terms[CUTS * i : CUTS * (i + 1)]) for i in each)
        total_a, total16_a, spill_a = add_up(row_offsets, first)
        spill_in_a = step(spill_a, "tile", 1)
        if iteration + 1 < ITERS:
            total_in_a = step(total16_a, "tile", -1)
            out = middle(
                row_offsets, object_slices, margins[0], total_a, spill_a, spill_in_a,
                total_in_a, *second
            )
            own_a, cut_a, (total_b, total16_b, spill_b) = out[0], out[1 : 1 + CUTS], out[1 + CUTS :]
            spill_in_b = step(spill_b, "tile", 1)
            total_in_b = step(total16_b, "tile", -1)
            windows = exchange(cut_a)
            own_b, *cut_b = update(
                1, row_offsets, object_slices, margins[1], total_b, spill_b, spill_in_b, total_in_b
            )
            windows += exchange(cut_b)
    total_b, _, spill_b = add_up(row_offsets, second)
    spill_in_b = step(spill_b, "tile", 1)
    return finish(own_a, total_a, spill_in_a, own_b, total_b, spill_in_b)


def solution(mesh):
    in_specs = (
        P("cuts", None, "tile", None),
        P(),
        P("tile"),
        P("tile"),
        P("tile"),
        P("tile", None, None),
    )
    out_specs = P("cuts", None, "tile", None)
    return jax.shard_map(run, mesh=mesh, in_specs=in_specs, out_specs=out_specs, check_vma=False)
```
